32 devices in a mesh: group: 2 (over x), trade: 16 (over z, y, core).
Axes of the slice: x: 2, y: 2, z: 4, core: 2. Of those that a mesh axis runs over, the one named last changes fastest.
Arguments:
- factors: bfloat16 [128, 128], P(('group', 'trade')), parts along dimension 0, may hold values from -6 to 6
- loadings: float32 [32, 16], replicated, may hold values from -1.5 to 1.5
- trade_coef: bfloat16 [65536, 256], P(('group', 'trade')), parts along dimension 0, may hold values from -0.75 to 0.75
- basis_size: int32 [65536], P(('group', 'trade')), parts along dimension 0, may hold values from 4 to 32
- set_ids: int32 [65536], P(('group', 'trade')), parts along dimension 0, may hold values from 0 to 31
- live_count: int32 [32], P(('group', 'trade')), parts along dimension 0, may hold values from 1 to 2047, as said below
- netting_row: int32 [64], P('group'), parts along dimension 0, may hold values from 0 to 31, each once
- threshold: float32 [64], P(('group', 'trade')), parts along dimension 0, may hold values from 0.5 to 8
- margin_start: float32 [64, 64], P(('group', 'trade')), parts along dimension 0, may hold values from 0 to 3
Outputs:
- expected: float32 [64, 8], P(('group', 'trade')), parts along dimension 0
The draws below stay inside these ranges and needn't reach their ends.
There are 2 independent parts, one for each index of `group`. The reference program is written for one: setup_inputs(seed, part) draws one part's arguments, and reference() takes and returns one part's arrays. A program takes and returns all parts, laid end to end along the dimension named above; an argument that names none is the same for every part. Nothing has to cross between parts.
Inputs may be any that keep to these rules, and one draw needn't show every extreme that they name: `live_count`: blocks b and b + 8 hold exactly 2048 live trades together.
All inputs are finite; a program needn't handle non-finite values.
Results may differ from the reference program's by a relative error of at most 0.00035.
Values may be sent and summed in bfloat16 or wider, within the bound.
A program may use at most 64 MiB of HBM per device.

```python
import math
import jax
import jax.numpy as jnp
import numpy as np
from jax import lax

F = 16
K = 32
DATES = 8
LAG = 2
AVG = 1024
SLOTS = 2048
BLOCKS = 16
TRADES = 32768
P_SIZE = 64
NS = 32


def draw_live_count(key, part):
    half_blocks = BLOCKS // 2
    first_key, second_key = jax.random.split(jax.random.fold_in(key, 11))
    lower = jax.random.randint(first_key, (half_blocks,), 1, 2 * AVG, dtype=jnp.int32)
    heavy = jax.random.randint(second_key, (), 0, half_blocks, dtype=jnp.int32)
    lower = jnp.where(jnp.arange(half_blocks, dtype=jnp.int32) == heavy, 2 * AVG - 1, lower)
    return jnp.concatenate([lower, 2 * AVG - lower]).astype(jnp.int32)


def set_ends(result, rng, smallest, top_value):
    spot = [jax.random.randint(jax.random.fold_in(rng, axis), (), 0, length) for axis, length in enumerate(result.shape)]
    widest = result.shape.index(max(result.shape))
    neighbour = spot[:widest] + [(spot[widest] + 1) % result.shape[widest]] + spot[widest + 1:]
    return result.at[tuple(spot)].set(smallest).at[tuple(neighbour)].set(top_value)


def block_levels(own_key, shape, shards, smallest, top_value):
    level = 1.0
    for axis_at, parts in shards:
        draws = jax.random.uniform(jax.random.fold_in(jax.random.fold_in(own_key, 6), axis_at), (parts,), jnp.float32, smallest / len(shards), top_value / len(shards))
        level = level * jnp.repeat(jnp.exp(draws), shape[axis_at] // parts).reshape((-1,) + (1,) * (len(shape) - 1 - axis_at))
    return level


def rank_table(count, slope):
    portions = [(1 << 20) // math.isqrt(standing ** slope) + 1 for standing in range(1, count + 1)]
    spread = 1 + sum(portions) // (1 << 30)
    return np.cumsum(np.array([max(1, weight // spread) for weight in portions]))


def ranked_ids(stream_key, extent, number_of, lean):
    listing = rank_table(number_of, lean)
    lot = jax.random.randint(jax.random.fold_in(stream_key, 1), extent, 0, int(listing[number_of - 1]))
    grade = jnp.searchsorted(jnp.asarray(listing, jnp.int32), lot, side="right")
    return jax.random.permutation(jax.random.fold_in(stream_key, 2), number_of)[grade].astype(jnp.int32)


def scatter_about(key, dims, width, most, shards=(), kind=jnp.bfloat16):
    level = block_levels(key, dims, shards, -0.22, 0.18) if shards else 1.0
    entries = jax.random.normal(key, dims, jnp.float32) * width * level
    return jnp.minimum(jnp.maximum(entries, -most), most).astype(kind)


def setup_inputs(seed: int = 0, part: int = 0) -> dict:
    splits = jax.random.split(jax.random.key(seed), 10)
    own_keys = jax.random.split(jax.random.fold_in(splits[9], part), 10)
    factors = scatter_about(own_keys[0], (P_SIZE, DATES * F), 1.0, 6.0, ((0, 16),))
    loadings = scatter_about(splits[1], (K, F), F ** -0.5, 1.5, (), jnp.float32)
    trade_coef = scatter_about(own_keys[2], (TRADES, DATES * K), 0.05, 0.75, ((0, 16),))
    basis_size = set_ends(jax.random.randint(own_keys[3], (TRADES,), 4, K + 1), jax.random.fold_in(own_keys[3], 1), 4, K).astype(jnp.int32)
    set_ids = set_ends(ranked_ids(own_keys[4], (TRADES,), NS, 1), jax.random.fold_in(own_keys[4], 3), 0, NS - 1).astype(jnp.int32)
    live_count = draw_live_count(jax.random.fold_in(jax.random.fold_in(splits[9], part), 71), part)
    netting_row = jax.random.permutation(own_keys[6], NS).astype(jnp.int32)
    threshold = jnp.clip(jnp.exp(math.log(8.0) - 2.7725887 * jax.random.uniform(own_keys[7], (NS,), jnp.float32) ** block_levels(own_keys[7], (NS,), ((0, 16),), -0.2, 0.2)), 0.5, 8.0)
    margin_start = jnp.clip(3.0 * jax.random.uniform(own_keys[8], (NS, P_SIZE), jnp.float32) ** block_levels(own_keys[8], (NS, P_SIZE), ((0, 16),), -0.2, 0.2), 0.0, 3.0)
    return {"factors": factors, "loadings": loadings, "trade_coef": trade_coef, "basis_size": basis_size, "set_ids": set_ids, "live_count": live_count, "netting_row": netting_row, "threshold": threshold, "margin_start": margin_start}


def reference(factors, loadings, trade_coef, basis_size, set_ids, live_count, netting_row, threshold, margin_start):
    path_total = factors.shape[0]
    set_total = netting_row.shape[0]
    factor_cube = factors.astype(jnp.float32).reshape(path_total, DATES, F)
    basis_table = jnp.einsum("pdf,kf->pdk", factor_cube, loadings, precision=lax.Precision.HIGHEST)
    basis_table = jnp.tanh(basis_table).astype(jnp.bfloat16)
    basis_wide = basis_table.astype(jnp.float32)
    trade_rows = netting_row[set_ids].astype(jnp.int32)
    basis_index = jnp.arange(K, dtype=jnp.int32)
    slot_index = jnp.arange(SLOTS, dtype=jnp.int32)

    def add_block(block_index, running):
        first_row = (block_index * SLOTS).astype(jnp.int32)
        coef_block = lax.dynamic_slice_in_dim(trade_coef, first_row, SLOTS, 0).reshape(SLOTS, DATES, K)
        sizes_block = lax.dynamic_slice_in_dim(basis_size, first_row, SLOTS, 0)
        rows_block = lax.dynamic_slice_in_dim(trade_rows, first_row, SLOTS, 0)
        live_now = live_count[block_index]
        keep_mask = (basis_index[None, :] < sizes_block[:, None]) & (slot_index < live_now)[:, None]
        coef_used = jnp.where(keep_mask[:, None, :], coef_block, jnp.zeros_like(coef_block)).astype(jnp.bfloat16)
        values = jnp.einsum("tdk,pdk->tdp", coef_used.astype(jnp.float32), basis_wide)
        values = values.astype(jnp.bfloat16).astype(jnp.float32).reshape(SLOTS, DATES * path_total)
        return running + jax.ops.segment_sum(values, rows_block, num_segments=set_total)

    running = jnp.zeros((set_total, DATES * path_total), jnp.float32)
    running = lax.fori_loop(0, BLOCKS, add_block, running)
    netted = running.reshape(set_total, DATES, path_total)
    margin = jnp.maximum(netted[:, : DATES - LAG] - threshold[:, None, None], 0.0)
    held = jnp.broadcast_to(margin_start[:, None, :], (set_total, LAG, path_total))
    collateral = jnp.concatenate([held, margin], axis=1)
    shortfall = jnp.maximum(netted - collateral, 0.0)
    return jnp.sum(shortfall, axis=2) / path_total
```

```python
import functools

import jax
import jax.numpy as jnp
from jax import lax
from jax.experimental import pallas as pl
from jax.experimental.pallas import tpu as pltpu
from jax.sharding import PartitionSpec as P

F = 16
K = 32
DATES = 8
LAG = 2
LANES = 128
CHUNK = 256
COLS = 512
MESH = pl.DeviceIdType.MESH
f32 = jnp.float32
bf16 = jnp.bfloat16


def iota(shape, axis):
    return lax.broadcasted_iota(jnp.int32, shape, axis)


def kernel(
    n,
    factors,
    loadings,
    trade_coef,
    basis_size,
    set_ids,
    live_count,
    netting_row,
    threshold,
    margin_start,
    out,
    fact,
    load_v,
    coef_v,
    size_v,
    ids_v,
    live_s,
    nrow_v,
    thr_s,
    marg_v,
    split,
    onehot,
    spread,
    basis,
    held,
    acc,
    part,
    recv,
    in_sem,
    gs_sem,
    gr_sem,
    ss_sem,
    sr_sem,
):
    me = lax.axis_index("trade")
    rows = fact.shape[1]
    paths = n * rows
    rep = max(1, LANES // paths)
    width = rep * paths
    slots = coef_v.shape[0]
    owned = recv.shape[1]
    sets = n * owned

    def peer(k):
        return lax.rem(me + k, n)

    def each_peer(step):
        lax.fori_loop(1, n, lambda k, c: (step(peer(k)), c)[1], 0)

    def local(src, dst, i):
        return pltpu.make_async_copy(src, dst, in_sem.at[i])

    barrier = pltpu.get_barrier_semaphore()
    each_peer(lambda j: pl.semaphore_signal(barrier, inc=1, device_id={"trade": j}, device_id_type=MESH))

    copies = [
        local(factors, fact.at[me], 0),
        local(loadings, load_v, 1),
        local(basis_size, size_v, 2),
        local(live_count, live_s, 3),
        local(netting_row, nrow_v, 4),
        local(set_ids, ids_v, 5),
        local(threshold, thr_s, 6),
        local(margin_start, marg_v, 7),
        local(trade_coef, coef_v, 8),
    ]
    for copy in copies:
        copy.start()
    copies[0].wait()
    pl.semaphore_wait(barrier, n - 1)

    def gather(j, slot):
        return pltpu.make_async_remote_copy(
            src_ref=fact.at[me],
            dst_ref=fact.at[me],
            send_sem=gs_sem.at[j],
            recv_sem=gr_sem.at[slot],
            device_id={"trade": j},
            device_id_type=MESH,
        )

    each_peer(lambda j: gather(j, me).start())

    copies[1].wait()
    tiled = (iota((F, LANES), 1) % F == iota((F, LANES), 0)).astype(f32).astype(bf16)
    diag = iota((DATES * K, LANES), 0) // K == iota((DATES * K, LANES), 1) // F
    rest = load_v[...]
    for i in range(3):
        piece = rest.astype(bf16)
        rest = rest - piece.astype(f32)
        wide = jnp.dot(piece, tiled, preferred_element_type=f32)
        wide = jnp.concatenate([wide] * DATES, axis=0)
        split[i] = jnp.where(diag, wide, 0.0).astype(bf16)
    basis[...] = jnp.zeros(basis.shape, bf16)

    copies[4].wait()
    copies[5].wait()
    found = nrow_v[...] == iota((sets, sets), 0)
    owner_set = jnp.sum(jnp.where(found, iota((sets, sets), 1), 0).astype(f32), axis=1, keepdims=True)
    owner_set = owner_set.astype(jnp.int32)
    for c in range(slots // CHUNK):
        cut = slice(c * CHUNK, (c + 1) * CHUNK)
        onehot[:, cut] = (ids_v[:, cut] == owner_set).astype(f32).astype(bf16)

    copies[7].wait()
    for i in range(LAG):
        held[:, i * paths : (i + 1) * paths] = marg_v[...]

    for i in (2, 3, 8):
        copies[i].wait()
    live_now = live_s[0]
    slot_index = iota(size_v.shape, 0) * LANES + iota(size_v.shape, 1)
    used = jnp.where(slot_index < live_now, size_v[...], 0).astype(f32)
    basis_index = (iota((LANES, LANES), 1) % K).astype(f32)
    for c in range(slots // LANES):
        limit = jnp.broadcast_to(used[c : c + 1], (LANES, LANES)).T
        keep = basis_index < limit
        cut = slice(c * LANES, (c + 1) * LANES)
        for h in range(0, DATES * K, LANES):
            side = slice(h, h + LANES)
            coef_v[cut, side] = jnp.where(keep, coef_v[cut, side].astype(f32), 0.0).astype(bf16)
    copies[6].wait()

    each_peer(lambda j: gather(j, j).wait_recv())

    for j in range(n):
        block = fact[j].astype(f32)
        for i in range(rep):
            at = i * paths + j * rows
            spread[at : at + rows] = block
    table = spread[...].astype(bf16)
    dims = (((1,), (1,)), ((), ()))
    loaded = lax.dot_general(split[2], table, dims, preferred_element_type=f32)
    loaded += lax.dot_general(split[1], table, dims, preferred_element_type=f32)
    loaded += lax.dot_general(split[0], table, dims, preferred_element_type=f32)
    bent = jnp.tanh(loaded)
    tall = rep * K
    pair = iota((tall, width), 0) // K == iota((tall, width), 1) // paths
    for j in range(DATES // rep):
        strip = jnp.where(pair, bent[j * tall : (j + 1) * tall], 0.0).astype(bf16)
        basis[j * tall : (j + 1) * tall, j * width : (j + 1) * width] = strip

    def block_sums(right):
        total = None
        for c in range(slots // CHUNK):
            cut = slice(c * CHUNK, (c + 1) * CHUNK)
            values = jnp.dot(coef_v[cut], right, preferred_element_type=f32).astype(bf16)
            term = jnp.dot(onehot[:, cut], values, preferred_element_type=f32)
            total = term if total is None else total + term
        return total

    blocks = acc.shape[1] // COLS
    if blocks == 1:
        acc[...] = block_sums(basis[...])
    else:

        def one(b, carry):
            side = pl.ds(pl.multiple_of(b * COLS, COLS), COLS)
            acc[:, side] = block_sums(basis[:, side])
            return carry

        lax.fori_loop(0, blocks, one, 0)
    for j in range(n):
        part[j] = acc[j * owned : (j + 1) * owned]

    def scatter(j, slot):
        return pltpu.make_async_remote_copy(
            src_ref=part.at[j],
            dst_ref=recv.at[me],
            send_sem=ss_sem.at[j],
            recv_sem=sr_sem.at[slot],
            device_id={"trade": j},
            device_id_type=MESH,
        )

    each_peer(lambda j: scatter(j, me).start())
    recv[me] = part[me]
    each_peer(lambda j: scatter(j, j).wait_recv())

    netted = recv[0]
    for j in range(1, n):
        netted = netted + recv[j]
    row_at = iota((owned, 1), 0)
    limits = jnp.zeros((owned, 1), f32)
    for r in range(owned):
        limits = jnp.where(row_at == r, thr_s[r], limits)
    first = LAG * paths
    margin = jnp.maximum(netted[:, : (DATES - LAG) * paths] - limits, 0.0)
    head = jnp.maximum(netted[:, :first] - held[...], 0.0)
    tail = jnp.maximum(netted[:, first:] - margin, 0.0)
    result = jnp.zeros(out.shape, f32)
    lane_date = iota((owned, width), 1) // paths
    column = iota(out.shape, 1)
    for j in range(DATES // rep):
        at = j * width
        block = head[:, at : at + width] if at < first else tail[:, at - first : at - first + width]
        for i in range(rep):
            own = jnp.where(lane_date == i, block, 0.0) if rep > 1 else block
            result = jnp.where(column == j * rep + i, jnp.sum(own, axis=1, keepdims=True), result)
    out[...] = result
    each_peer(lambda j: gather(j, j).wait_send())
    each_peer(lambda j: scatter(j, j).wait_send())


def body(n, factors, loadings, trade_coef, basis_size, set_ids, live_count, netting_row, threshold, margin_start):
    rows = factors.shape[0]
    paths = n * rows
    rep = max(1, LANES // paths)
    slots = trade_coef.shape[0]
    sets = netting_row.shape[0]
    owned = threshold.shape[0]
    wide = DATES * paths
    hbm = pl.BlockSpec(memory_space=pltpu.MemorySpace.HBM)
    total = pl.pallas_call(
        functools.partial(kernel, n),
        out_shape=jax.ShapeDtypeStruct((owned, DATES), f32),
        in_specs=[hbm] * 9,
        out_specs=pl.BlockSpec(memory_space=pltpu.VMEM),
        scratch_shapes=[
            pltpu.VMEM((n, rows, DATES * F), bf16),
            pltpu.VMEM((K, F), f32),
            pltpu.VMEM((slots, DATES * K), bf16),
            pltpu.VMEM((slots // LANES, LANES), jnp.int32),
            pltpu.VMEM((1, slots), jnp.int32),
            pltpu.SMEM((1,), jnp.int32),
            pltpu.VMEM((1, sets), jnp.int32),
            pltpu.SMEM((owned,), f32),
            pltpu.VMEM((owned, paths), f32),
            pltpu.VMEM((3, DATES * K, DATES * F), bf16),
            pltpu.VMEM((sets, slots), bf16),
            pltpu.VMEM((rep * paths, DATES * F), f32),
            pltpu.VMEM((DATES * K, wide), bf16),
            pltpu.VMEM((owned, LAG * paths), f32),
            pltpu.VMEM((sets, wide), f32),
            pltpu.VMEM((n, owned, wide), f32),
            pltpu.VMEM((n, owned, wide), f32),
            pltpu.SemaphoreType.DMA((9,)),
            pltpu.SemaphoreType.DMA((n,)),
            pltpu.SemaphoreType.DMA((n,)),
            pltpu.SemaphoreType.DMA((n,)),
            pltpu.SemaphoreType.DMA((n,)),
        ],
        compiler_params=pltpu.CompilerParams(
            collective_id=0, has_side_effects=True, vmem_limit_bytes=48 * 2**20
        ),
    )(
        factors,
        loadings,
        trade_coef,
        basis_size.reshape(slots // LANES, LANES),
        set_ids.reshape(1, slots),
        live_count,
        netting_row.reshape(1, sets),
        threshold,
        margin_start,
    )
    return total / paths


def solution(mesh):
    return jax.shard_map(
        functools.partial(body, mesh.shape["trade"]),
        mesh=mesh,
        in_specs=(
            P(("group", "trade"), None),
            P(),
            P(("group", "trade"), None),
            P(("group", "trade")),
            P(("group", "trade")),
            P(("group", "trade")),
            P("group"),
            P(("group", "trade")),
            P(("group", "trade"), None),
        ),
        out_specs=P(("group", "trade"), None),
        check_vma=False,
    )
```

```python
import functools

import jax
import jax.numpy as jnp
from jax import lax
from jax.experimental import pallas as pl
from jax.experimental.pallas import tpu as pltpu
from jax.sharding import PartitionSpec as P

F = 16
K = 32
DATES = 8
LAG = 2
LANES = 128
CHUNK = 256
COLS = 512
MESH = pl.DeviceIdType.MESH
f32 = jnp.float32
bf16 = jnp.bfloat16


def iota(shape, axis):
    return lax.broadcasted_iota(jnp.int32, shape, axis)


def kernel(
    n,
    factors,
    loadings,
    trade_coef,
    basis_size,
    set_ids,
    live_count,
    netting_row,
    threshold,
    margin_start,
    out,
    fact,
    load_v,
    coef_v,
    size_v,
    ids_v,
    nrow_v,
    thr_s,
    marg_v,
    split,
    onehot,
    spread,
    basis,
    held,
    acc,
    part,
    recv,
    in_sem,
    gs_sem,
    gr_sem,
    ss_sem,
    sr_sem,
):
    me = lax.axis_index("trade")
    rows = fact.shape[1]
    paths = n * rows
    rep = max(1, LANES // paths)
    width = rep * paths
    slots = coef_v.shape[0]
    owned = recv.shape[1]
    sets = n * owned

    def peer(k):
        return lax.rem(me + k, n)

    def each_peer(step):
        lax.fori_loop(1, n, lambda k, c: (step(peer(k)), c)[1], 0)

    def local(src, dst, i):
        return pltpu.make_async_copy(src, dst, in_sem.at[i])

    barrier = pltpu.get_barrier_semaphore()
    each_peer(lambda j: pl.semaphore_signal(barrier, inc=1, device_id={"trade": j}, device_id_type=MESH))

    copies = [
        local(factors, fact.at[me], 0),
        local(loadings, load_v, 1),
        local(basis_size, size_v, 2),
        local(threshold, thr_s, 3),
        local(netting_row, nrow_v, 4),
        local(set_ids, ids_v, 5),
        local(margin_start, marg_v, 6),
        local(trade_coef, coef_v, 7),
    ]
    for copy in copies:
        copy.start()
    copies[0].wait()
    pl.semaphore_wait(barrier, n - 1)

    def gather(j, slot):
        return pltpu.make_async_remote_copy(
            src_ref=fact.at[me],
            dst_ref=fact.at[me],
            send_sem=gs_sem.at[j],
            recv_sem=gr_sem.at[slot],
            device_id={"trade": j},
            device_id_type=MESH,
        )

    each_peer(lambda j: gather(j, me).start())

    copies[1].wait()
    tiled = (iota((F, LANES), 1) % F == iota((F, LANES), 0)).astype(f32).astype(bf16)
    diag = iota((DATES * K, LANES), 0) // K == iota((DATES * K, LANES), 1) // F
    rest = load_v[...]
    for i in range(3):
        piece = rest.astype(bf16)
        rest = rest - piece.astype(f32)
        wide = lax.dot_general(piece, tiled, (((0,), (0,)), ((), ())), preferred_element_type=f32)
        wide = jnp.concatenate([wide] * DATES, axis=0)
        split[i] = jnp.where(diag, wide, 0.0).astype(bf16)
    basis[...] = jnp.zeros(basis.shape, bf16)

    copies[4].wait()
    copies[5].wait()
    found = nrow_v[...] == iota((sets, sets), 0)
    owner_set = jnp.sum(jnp.where(found, iota((sets, sets), 1), 0).astype(f32), axis=1, keepdims=True)
    owner_set = owner_set.astype(jnp.int32)
    for c in range(slots // CHUNK):
        cut = slice(c * CHUNK, (c + 1) * CHUNK)
        onehot[:, cut] = (ids_v[:, cut] == owner_set).astype(f32).astype(bf16)

    copies[6].wait()
    for i in range(LAG):
        held[:, i * paths : (i + 1) * paths] = marg_v[...]

    for i in (2, 3, 7):
        copies[i].wait()
    live_now = live_count[0]
    slot_index = iota(size_v.shape, 0) * LANES + iota(size_v.shape, 1)
    used = jnp.where(slot_index < live_now, size_v[...], 0).astype(f32)
    basis_index = (iota((LANES, LANES), 1) % K).astype(f32)
    for c in range(slots // LANES):
        limit = jnp.broadcast_to(used[c : c + 1], (LANES, LANES)).T
        keep = basis_index < limit
        cut = slice(c * LANES, (c + 1) * LANES)
        for h in range(0, DATES * K, LANES):
            side = slice(h, h + LANES)
            coef_v[cut, side] = jnp.where(keep, coef_v[cut, side].astype(f32), 0.0).astype(bf16)

    each_peer(lambda j: gather(j, j).wait_recv())

    for j in range(n):
        block = fact[j].astype(f32)
        for i in range(rep):
            at = i * paths + j * rows
            spread[at : at + rows] = block
    table = spread[...].astype(bf16)
    dims = (((1,), (1,)), ((), ()))
    loaded = lax.dot_general(split[2], table, dims, preferred_element_type=f32)
    loaded += lax.dot_general(split[1], table, dims, preferred_element_type=f32)
    loaded += lax.dot_general(split[0], table, dims, preferred_element_type=f32)
    bent = jnp.tanh(loaded)
    tall = rep * K
    pair = iota((tall, width), 0) // K == iota((tall, width), 1) // paths
    for j in range(DATES // rep):
        strip = jnp.where(pair, bent[j * tall : (j + 1) * tall], 0.0).astype(bf16)
        basis[j * tall : (j + 1) * tall, j * width : (j + 1) * width] = strip

    def block_sums(right):
        total = None
        for c in range(slots // CHUNK):
            cut = slice(c * CHUNK, (c + 1) * CHUNK)
            values = jnp.dot(coef_v[cut], right, preferred_element_type=f32).astype(bf16)
            term = jnp.dot(onehot[:, cut], values, preferred_element_type=f32)
            total = term if total is None else total + term
        return total

    blocks = acc.shape[1] // COLS
    if blocks == 1:
        acc[...] = block_sums(basis[...])
    else:

        def one(b, carry):
            side = pl.ds(pl.multiple_of(b * COLS, COLS), COLS)
            acc[:, side] = block_sums(basis[:, side])
            return carry

        lax.fori_loop(0, blocks, one, 0)
    for j in range(n):
        part[j] = acc[j * owned : (j + 1) * owned]

    def scatter(j, slot):
        return pltpu.make_async_remote_copy(
            src_ref=part.at[j],
            dst_ref=recv.at[me],
            send_sem=ss_sem.at[j],
            recv_sem=sr_sem.at[slot],
            device_id={"trade": j},
            device_id_type=MESH,
        )

    each_peer(lambda j: scatter(j, me).start())
    recv[me] = part[me]
    each_peer(lambda j: scatter(j, j).wait_recv())

    netted = recv[0]
    for j in range(1, n):
        netted = netted + recv[j]
    row_at = iota((owned, 1), 0)
    limits = jnp.zeros((owned, 1), f32)
    for r in range(owned):
        limits = jnp.where(row_at == r, thr_s[r], limits)
    first = LAG * paths
    margin = jnp.maximum(netted[:, : (DATES - LAG) * paths] - limits, 0.0)
    head = jnp.maximum(netted[:, :first] - held[...], 0.0)
    tail = jnp.maximum(netted[:, first:] - margin, 0.0)
    result = jnp.zeros(out.shape, f32)
    lane_date = iota((owned, width), 1) // paths
    column = iota(out.shape, 1)
    for j in range(DATES // rep):
        at = j * width
        block = head[:, at : at + width] if at < first else tail[:, at - first : at - first + width]
        for i in range(rep):
            own = jnp.where(lane_date == i, block, 0.0) if rep > 1 else block
            result = jnp.where(column == j * rep + i, jnp.sum(own, axis=1, keepdims=True), result)
    out[...] = result
    each_peer(lambda j: gather(j, j).wait_send())
    each_peer(lambda j: scatter(j, j).wait_send())


def body(n, factors, loadings, trade_coef, basis_size, set_ids, live_count, netting_row, threshold, margin_start):
    rows = factors.shape[0]
    paths = n * rows
    rep = max(1, LANES // paths)
    slots = trade_coef.shape[0]
    sets = netting_row.shape[0]
    owned = threshold.shape[0]
    wide = DATES * paths
    hbm = pl.BlockSpec(memory_space=pltpu.MemorySpace.HBM)
    total = pl.pallas_call(
        functools.partial(kernel, n),
        out_shape=jax.ShapeDtypeStruct((owned, DATES), f32),
        in_specs=[hbm] * 5 + [pl.BlockSpec(memory_space=pltpu.SMEM)] + [hbm] * 3,
        out_specs=pl.BlockSpec(memory_space=pltpu.VMEM),
        scratch_shapes=[
            pltpu.VMEM((n, rows, DATES * F), bf16),
            pltpu.VMEM((F, K), f32),
            pltpu.VMEM((slots, DATES * K), bf16),
            pltpu.VMEM((slots // LANES, LANES), jnp.int32),
            pltpu.VMEM((1, slots), jnp.int32),
            pltpu.VMEM((1, sets), jnp.int32),
            pltpu.SMEM((owned,), f32),
            pltpu.VMEM((owned, paths), f32),
            pltpu.VMEM((3, DATES * K, DATES * F), bf16),
            pltpu.VMEM((sets, slots), bf16),
            pltpu.VMEM((rep * paths, DATES * F), f32),
            pltpu.VMEM((DATES * K, wide), bf16),
            pltpu.VMEM((owned, LAG * paths), f32),
            pltpu.VMEM((sets, wide), f32),
            pltpu.VMEM((n, owned, wide), f32),
            pltpu.VMEM((n, owned, wide), f32),
            pltpu.SemaphoreType.DMA((8,)),
            pltpu.SemaphoreType.DMA((n,)),
            pltpu.SemaphoreType.DMA((n,)),
            pltpu.SemaphoreType.DMA((n,)),
            pltpu.SemaphoreType.DMA((n,)),
        ],
        compiler_params=pltpu.CompilerParams(
            collective_id=0, has_side_effects=True, vmem_limit_bytes=67043328
        ),
    )(
        factors,
        loadings.T,
        trade_coef,
        basis_size.reshape(slots // LANES, LANES),
        set_ids.reshape(1, slots),
        live_count,
        netting_row.reshape(1, sets),
        threshold,
        margin_start,
    )
    return total / paths


def solution(mesh):
    return jax.shard_map(
        functools.partial(body, mesh.shape["trade"]),
        mesh=mesh,
        in_specs=(
            P(("group", "trade"), None),
            P(),
            P(("group", "trade"), None),
            P(("group", "trade")),
            P(("group", "trade")),
            P(("group", "trade")),
            P("group"),
            P(("group", "trade")),
            P(("group", "trade"), None),
        ),
        out_specs=P(("group", "trade"), None),
        check_vma=False,
    )
```

```python
import functools

import jax
import jax.numpy as jnp
from jax import lax
from jax.experimental import pallas as pl
from jax.experimental.pallas import tpu as pltpu
from jax.sharding import PartitionSpec as P

F = 16
K = 32
DATES = 8
LAG = 2
LANES = 128
CHUNK = 256
COLS = 512
MESH = pl.DeviceIdType.MESH
f32 = jnp.float32
bf16 = jnp.bfloat16


def iota(shape, axis):
    return lax.broadcasted_iota(jnp.int32, shape, axis)


def kernel(
    n,
    factors,
    loadings,
    trade_coef,
    basis_size,
    set_ids,
    live_count,
    netting_row,
    threshold,
    margin_start,
    out,
    fact,
    load_v,
    coef_v,
    size_v,
    ids_v,
    nrow_v,
    thr_s,
    marg_v,
    split,
    onehot,
    spread,
    basis,
    held,
    acc,
    part,
    recv,
    in_sem,
    gs_sem,
    gr_sem,
    ss_sem,
    sr_sem,
):
    me = lax.axis_index("trade")
    rows = fact.shape[1]
    paths = n * rows
    rep = max(1, LANES // paths)
    width = rep * paths
    slots = coef_v.shape[0]
    owned = recv.shape[1]
    sets = n * owned

    def peer(k):
        return lax.rem(me + k, n)

    def each_peer(step):
        lax.fori_loop(1, n, lambda k, c: (step(peer(k)), c)[1], 0)

    def local(src, dst, i):
        return pltpu.make_async_copy(src, dst, in_sem.at[i])

    barrier = pltpu.get_barrier_semaphore()
    each_peer(lambda j: pl.semaphore_signal(barrier, inc=1, device_id={"trade": j}, device_id_type=MESH))

    copies = [
        local(factors, fact.at[me], 0),
        local(loadings, load_v, 1),
        local(basis_size, size_v, 2),
        local(threshold, thr_s, 3),
        local(netting_row, nrow_v, 4),
        local(set_ids, ids_v, 5),
        local(margin_start, marg_v, 6),
        local(trade_coef, coef_v, 7),
    ]
    for copy in copies:
        copy.start()
    copies[0].wait()
    pl.semaphore_wait(barrier, n - 1)

    def gather(j, slot):
        return pltpu.make_async_remote_copy(
            src_ref=fact.at[me],
            dst_ref=fact.at[me],
            send_sem=gs_sem.at[j],
            recv_sem=gr_sem.at[slot],
            device_id={"trade": j},
            device_id_type=MESH,
        )

    each_peer(lambda j: gather(j, me).start())

    copies[1].wait()
    tiled = (iota((F, LANES), 1) % F == iota((F, LANES), 0)).astype(f32).astype(bf16)
    diag = iota((DATES * K, LANES), 0) // K == iota((DATES * K, LANES), 1) // F
    rest = load_v[...]
    for i in range(3):
        piece = rest.astype(bf16)
        rest = rest - piece.astype(f32)
        wide = lax.dot_general(piece, tiled, (((0,), (0,)), ((), ())), preferred_element_type=f32)
        wide = jnp.concatenate([wide] * DATES, axis=0)
        split[i] = jnp.where(diag, wide, 0.0).astype(bf16)
    basis[...] = jnp.zeros(basis.shape, bf16)

    copies[4].wait()
    copies[5].wait()
    found = nrow_v[...] == iota((sets, sets), 0)
    owner_set = jnp.sum(jnp.where(found, iota((sets, sets), 1), 0).astype(f32), axis=1, keepdims=True)
    owner_set = owner_set.astype(jnp.int32)
    for c in range(slots // CHUNK):
        cut = slice(c * CHUNK, (c + 1) * CHUNK)
        onehot[:, cut] = (ids_v[:, cut] == owner_set).astype(f32).astype(bf16)

    copies[6].wait()
    for i in range(LAG):
        held[:, i * paths : (i + 1) * paths] = marg_v[...]

    for i in (2, 3, 7):
        copies[i].wait()
    live_now = live_count[0]
    slot_index = iota(size_v.shape, 0) * LANES + iota(size_v.shape, 1)
    used = jnp.where(slot_index < live_now, size_v[...], 0).astype(f32)
    basis_index = (iota((LANES, LANES), 1) % K).astype(f32)
    for c in range(slots // LANES):
        limit = jnp.broadcast_to(used[c : c + 1], (LANES, LANES)).T
        keep = basis_index < limit
        cut = slice(c * LANES, (c + 1) * LANES)
        for h in range(0, DATES * K, LANES):
            side = slice(h, h + LANES)
            coef_v[cut, side] = jnp.where(keep, coef_v[cut, side].astype(f32), 0.0).astype(bf16)

    each_peer(lambda j: gather(j, j).wait_recv())

    for j in range(n):
        block = fact[j].astype(f32)
        for i in range(rep):
            at = i * paths + j * rows
            spread[at : at + rows] = block
    table = spread[...].astype(bf16)
    dims = (((1,), (1,)), ((), ()))
    loaded = lax.dot_general(split[2], table, dims, preferred_element_type=f32)
    loaded += lax.dot_general(split[1], table, dims, preferred_element_type=f32)
    loaded += lax.dot_general(split[0], table, dims, preferred_element_type=f32)
    bent = jnp.tanh(loaded)
    tall = rep * K
    pair = iota((tall, width), 0) // K == iota((tall, width), 1) // paths
    for j in range(DATES // rep):
        strip = jnp.where(pair, bent[j * tall : (j + 1) * tall], 0.0).astype(bf16)
        basis[j * tall : (j + 1) * tall, j * width : (j + 1) * width] = strip

    def block_sums(right):
        total = None
        for c in range(slots // CHUNK):
            cut = slice(c * CHUNK, (c + 1) * CHUNK)
            values = jnp.dot(coef_v[cut], right, preferred_element_type=f32).astype(bf16)
            term = jnp.dot(onehot[:, cut], values, preferred_element_type=f32)
            total = term if total is None else total + term
        return total

    blocks = acc.shape[1] // COLS
    if blocks == 1:
        acc[...] = block_sums(basis[...])
    else:

        def one(b, carry):
            side = pl.ds(pl.multiple_of(b * COLS, COLS), COLS)
            acc[:, side] = block_sums(basis[:, side])
            return carry

        lax.fori_loop(0, blocks, one, 0)
    for j in range(n):
        part[j] = acc[j * owned : (j + 1) * owned]

    def scatter(j, slot):
        return pltpu.make_async_remote_copy(
            src_ref=part.at[j],
            dst_ref=recv.at[me],
            send_sem=ss_sem.at[j],
            recv_sem=sr_sem.at[slot],
            device_id={"trade": j},
            device_id_type=MESH,
        )

    each_peer(lambda j: scatter(j, me).start())
    recv[me] = part[me]
    each_peer(lambda j: scatter(j, j).wait_recv())

    netted = recv[0]
    for j in range(1, n):
        netted = netted + recv[j]
    row_at = iota((owned, 1), 0)
    limits = jnp.zeros((owned, 1), f32)
    for r in range(owned):
        limits = jnp.where(row_at == r, thr_s[r], limits)
    first = LAG * paths
    margin = jnp.maximum(netted[:, : (DATES - LAG) * paths] - limits, 0.0)
    head = jnp.maximum(netted[:, :first] - held[...], 0.0)
    tail = jnp.maximum(netted[:, first:] - margin, 0.0)
    result = jnp.zeros(out.shape, f32)
    lane_date = iota((owned, width), 1) // paths
    column = iota(out.shape, 1)
    for j in range(DATES // rep):
        at = j * width
        block = head[:, at : at + width] if at < first else tail[:, at - first : at - first + width]
        for i in range(rep):
            own = jnp.where(lane_date == i, block, 0.0) if rep > 1 else block
            result = jnp.where(column == j * rep + i, jnp.sum(own, axis=1, keepdims=True), result)
    out[...] = result
    each_peer(lambda j: gather(j, j).wait_send())
    each_peer(lambda j: scatter(j, j).wait_send())


def stay(x):
    return pltpu.with_memory_space_constraint(x, pltpu.MemorySpace.HBM)


def body(n, factors, loadings, trade_coef, basis_size, set_ids, live_count, netting_row, threshold, margin_start):
    rows = factors.shape[0]
    paths = n * rows
    rep = max(1, LANES // paths)
    slots = trade_coef.shape[0]
    sets = netting_row.shape[0]
    owned = threshold.shape[0]
    wide = DATES * paths
    hbm = pl.BlockSpec(memory_space=pltpu.MemorySpace.HBM)
    total = pl.pallas_call(
        functools.partial(kernel, n),
        out_shape=jax.ShapeDtypeStruct((owned, DATES), f32),
        in_specs=[hbm] * 5 + [pl.BlockSpec(memory_space=pltpu.SMEM)] + [hbm] * 3,
        out_specs=pl.BlockSpec(memory_space=pltpu.VMEM),
        scratch_shapes=[
            pltpu.VMEM((n, rows, DATES * F), bf16),
            pltpu.VMEM((F, K), f32),
            pltpu.VMEM((slots, DATES * K), bf16),
            pltpu.VMEM((slots // LANES, LANES), jnp.int32),
            pltpu.VMEM((1, slots), jnp.int32),
            pltpu.VMEM((1, sets), jnp.int32),
            pltpu.SMEM((owned,), f32),
            pltpu.VMEM((owned, paths), f32),
            pltpu.VMEM((3, DATES * K, DATES * F), bf16),
            pltpu.VMEM((sets, slots), bf16),
            pltpu.VMEM((rep * paths, DATES * F), f32),
            pltpu.VMEM((DATES * K, wide), bf16),
            pltpu.VMEM((owned, LAG * paths), f32),
            pltpu.VMEM((sets, wide), f32),
            pltpu.VMEM((n, owned, wide), f32),
            pltpu.VMEM((n, owned, wide), f32),
            pltpu.SemaphoreType.DMA((8,)),
            pltpu.SemaphoreType.DMA((n,)),
            pltpu.SemaphoreType.DMA((n,)),
            pltpu.SemaphoreType.DMA((n,)),
            pltpu.SemaphoreType.DMA((n,)),
        ],
        compiler_params=pltpu.CompilerParams(
            collective_id=0, has_side_effects=True, vmem_limit_bytes=48 * 2**20
        ),
    )(
        stay(factors),
        stay(loadings.T),
        stay(trade_coef),
        stay(basis_size.reshape(slots // LANES, LANES)),
        stay(set_ids.reshape(1, slots)),
        live_count,
        stay(netting_row.reshape(1, sets)),
        stay(threshold),
        stay(margin_start),
    )
    return total / paths


def solution(mesh):
    return jax.shard_map(
        functools.partial(body, mesh.shape["trade"]),
        mesh=mesh,
        in_specs=(
            P(("group", "trade"), None),
            P(),
            P(("group", "trade"), None),
            P(("group", "trade")),
            P(("group", "trade")),
            P(("group", "trade")),
            P("group"),
            P(("group", "trade")),
            P(("group", "trade"), None),
        ),
        out_specs=P(("group", "trade"), None),
        check_vma=False,
    )
```

```python
import functools

import jax
import jax.numpy as jnp
from jax import lax
from jax.experimental import pallas as pl
from jax.experimental.pallas import tpu as pltpu
from jax.sharding import PartitionSpec as P

F = 16
K = 32
DATES = 8
LAG = 2
LANES = 128
CHUNK = 256
COLS = 512
MESH = pl.DeviceIdType.MESH
f32 = jnp.float32
bf16 = jnp.bfloat16


def iota(shape, axis):
    return lax.broadcasted_iota(jnp.int32, shape, axis)


def kernel(
    n,
    factors,
    loadings,
    trade_coef,
    basis_size,
    set_ids,
    live_count,
    netting_row,
    threshold,
    margin_start,
    out,
    fact,
    load_v,
    coef_v,
    size_v,
    ids_v,
    nrow_v,
    thr_s,
    marg_v,
    split,
    onehot,
    spread,
    basis,
    held,
    acc,
    part,
    recv,
    in_sem,
    gs_sem,
    gr_sem,
    ss_sem,
    sr_sem,
):
    me = lax.axis_index("trade")
    rows = fact.shape[1]
    paths = n * rows
    rep = max(1, LANES // paths)
    width = rep * paths
    slots = coef_v.shape[0]
    owned = recv.shape[1]
    sets = n * owned

    def peer(k):
        return lax.rem(me + k, n)

    def each_peer(step):
        lax.fori_loop(1, n, lambda k, c: (step(peer(k)), c)[1], 0)

    def local(src, dst, i):
        return pltpu.make_async_copy(src, dst, in_sem.at[i])

    def settle(ref, sem):
        rest = ref.at[pl.ds(0, n - 1)]
        pltpu.make_async_copy(rest, rest, sem).wait()

    barrier = pltpu.get_barrier_semaphore()
    each_peer(lambda j: pl.semaphore_signal(barrier, inc=1, device_id={"trade": j}, device_id_type=MESH))

    own = local(factors, fact.at[me], 0)
    limit_copy = local(threshold, thr_s, 1)
    pairs = (
        (loadings, load_v),
        (basis_size, size_v),
        (netting_row, nrow_v),
        (set_ids, ids_v),
        (margin_start, marg_v),
        (trade_coef, coef_v),
    )
    copies = [local(src, dst, 2) for src, dst in pairs]
    for copy in (own, *copies, limit_copy):
        copy.start()
    own.wait()
    pl.semaphore_wait(barrier, n - 1)

    def gather(j):
        return pltpu.make_async_remote_copy(
            src_ref=fact.at[me],
            dst_ref=fact.at[me],
            send_sem=gs_sem,
            recv_sem=gr_sem,
            device_id={"trade": j},
            device_id_type=MESH,
        )

    each_peer(lambda j: gather(j).start())

    for copy in copies:
        copy.wait()
    limit_copy.wait()
    tiled = (iota((F, LANES), 1) % F == iota((F, LANES), 0)).astype(f32).astype(bf16)
    diag = iota((DATES * K, LANES), 0) // K == iota((DATES * K, LANES), 1) // F
    rest = load_v[...]
    for i in range(3):
        piece = rest.astype(bf16)
        rest = rest - piece.astype(f32)
        wide = lax.dot_general(piece, tiled, (((0,), (0,)), ((), ())), preferred_element_type=f32)
        wide = jnp.concatenate([wide] * DATES, axis=0)
        split[i] = jnp.where(diag, wide, 0.0).astype(bf16)
    basis[...] = jnp.zeros(basis.shape, bf16)

    found = nrow_v[...] == iota((sets, sets), 0)
    owner_set = jnp.sum(jnp.where(found, iota((sets, sets), 1), 0).astype(f32), axis=1, keepdims=True)
    owner_set = owner_set.astype(jnp.int32)
    for c in range(slots // CHUNK):
        cut = slice(c * CHUNK, (c + 1) * CHUNK)
        onehot[:, cut] = (ids_v[:, cut] == owner_set).astype(f32).astype(bf16)

    for i in range(LAG):
        held[:, i * paths : (i + 1) * paths] = marg_v[...]

    live_now = live_count[0]
    slot_index = iota(size_v.shape, 0) * LANES + iota(size_v.shape, 1)
    used = jnp.where(slot_index < live_now, size_v[...], 0).astype(f32)
    basis_index = (iota((LANES, LANES), 1) % K).astype(f32)
    for c in range(slots // LANES):
        limit = jnp.broadcast_to(used[c : c + 1], (LANES, LANES)).T
        keep = basis_index < limit
        cut = slice(c * LANES, (c + 1) * LANES)
        for h in range(0, DATES * K, LANES):
            side = slice(h, h + LANES)
            coef_v[cut, side] = jnp.where(keep, coef_v[cut, side].astype(f32), 0.0).astype(bf16)

    settle(fact, gr_sem)

    for j in range(n):
        block = fact[j].astype(f32)
        for i in range(rep):
            at = i * paths + j * rows
            spread[at : at + rows] = block
    table = spread[...].astype(bf16)
    dims = (((1,), (1,)), ((), ()))
    loaded = lax.dot_general(split[2], table, dims, preferred_element_type=f32)
    loaded += lax.dot_general(split[1], table, dims, preferred_element_type=f32)
    loaded += lax.dot_general(split[0], table, dims, preferred_element_type=f32)
    bent = jnp.tanh(loaded)
    tall = rep * K
    pair = iota((tall, width), 0) // K == iota((tall, width), 1) // paths
    for j in range(DATES // rep):
        strip = jnp.where(pair, bent[j * tall : (j + 1) * tall], 0.0).astype(bf16)
        basis[j * tall : (j + 1) * tall, j * width : (j + 1) * width] = strip

    def block_sums(right):
        total = None
        for c in range(slots // CHUNK):
            cut = slice(c * CHUNK, (c + 1) * CHUNK)
            values = jnp.dot(coef_v[cut], right, preferred_element_type=f32).astype(bf16)
            term = jnp.dot(onehot[:, cut], values, preferred_element_type=f32)
            total = term if total is None else total + term
        return total

    blocks = acc.shape[1] // COLS
    if blocks == 1:
        acc[...] = block_sums(basis[...])
    else:

        def one(b, carry):
            side = pl.ds(pl.multiple_of(b * COLS, COLS), COLS)
            acc[:, side] = block_sums(basis[:, side])
            return carry

        lax.fori_loop(0, blocks, one, 0)
    for j in range(n):
        part[j] = acc[j * owned : (j + 1) * owned]

    def scatter(j):
        return pltpu.make_async_remote_copy(
            src_ref=part.at[j],
            dst_ref=recv.at[me],
            send_sem=ss_sem,
            recv_sem=sr_sem,
            device_id={"trade": j},
            device_id_type=MESH,
        )

    each_peer(lambda j: scatter(j).start())
    recv[me] = part[me]
    settle(recv, sr_sem)

    netted = recv[0]
    for j in range(1, n):
        netted = netted + recv[j]
    row_at = iota((owned, 1), 0)
    limits = jnp.zeros((owned, 1), f32)
    for r in range(owned):
        limits = jnp.where(row_at == r, thr_s[r], limits)
    first = LAG * paths
    margin = jnp.maximum(netted[:, : (DATES - LAG) * paths] - limits, 0.0)
    head = jnp.maximum(netted[:, :first] - held[...], 0.0)
    tail = jnp.maximum(netted[:, first:] - margin, 0.0)
    result = jnp.zeros(out.shape, f32)
    lane_date = iota((owned, width), 1) // paths
    column = iota(out.shape, 1)
    for j in range(DATES // rep):
        at = j * width
        block = head[:, at : at + width] if at < first else tail[:, at - first : at - first + width]
        for i in range(rep):
            own = jnp.where(lane_date == i, block, 0.0) if rep > 1 else block
            result = jnp.where(column == j * rep + i, jnp.sum(own, axis=1, keepdims=True), result)
    out[...] = result
    settle(fact, gs_sem)
    settle(recv, ss_sem)


def stay(x):
    return pltpu.with_memory_space_constraint(x, pltpu.MemorySpace.HBM)


def body(n, factors, loadings, trade_coef, basis_size, set_ids, live_count, netting_row, threshold, margin_start):
    rows = factors.shape[0]
    paths = n * rows
    rep = max(1, LANES // paths)
    slots = trade_coef.shape[0]
    sets = netting_row.shape[0]
    owned = threshold.shape[0]
    wide = DATES * paths
    hbm = pl.BlockSpec(memory_space=pltpu.MemorySpace.HBM)
    total = pl.pallas_call(
        functools.partial(kernel, n),
        out_shape=jax.ShapeDtypeStruct((owned, DATES), f32),
        in_specs=[hbm] * 5 + [pl.BlockSpec(memory_space=pltpu.SMEM)] + [hbm] * 3,
        out_specs=pl.BlockSpec(memory_space=pltpu.VMEM),
        scratch_shapes=[
            pltpu.VMEM((n, rows, DATES * F), bf16),
            pltpu.VMEM((F, K), f32),
            pltpu.VMEM((slots, DATES * K), bf16),
            pltpu.VMEM((slots // LANES, LANES), jnp.int32),
            pltpu.VMEM((1, slots), jnp.int32),
            pltpu.VMEM((1, sets), jnp.int32),
            pltpu.SMEM((owned,), f32),
            pltpu.VMEM((owned, paths), f32),
            pltpu.VMEM((3, DATES * K, DATES * F), bf16),
            pltpu.VMEM((sets, slots), bf16),
            pltpu.VMEM((rep * paths, DATES * F), f32),
            pltpu.VMEM((DATES * K, wide), bf16),
            pltpu.VMEM((owned, LAG * paths), f32),
            pltpu.VMEM((sets, wide), f32),
            pltpu.VMEM((n, owned, wide), f32),
            pltpu.VMEM((n, owned, wide), f32),
            pltpu.SemaphoreType.DMA((3,)),
            pltpu.SemaphoreType.DMA,
            pltpu.SemaphoreType.DMA,
            pltpu.SemaphoreType.DMA,
            pltpu.SemaphoreType.DMA,
        ],
        compiler_params=pltpu.CompilerParams(
            collective_id=0, has_side_effects=True, vmem_limit_bytes=48 * 2**20
        ),
    )(
        stay(factors),
        stay(loadings.T),
        stay(trade_coef),
        stay(basis_size.reshape(slots // LANES, LANES)),
        stay(set_ids.reshape(1, slots)),
        live_count,
        stay(netting_row.reshape(1, sets)),
        stay(threshold),
        stay(margin_start),
    )
    return total / paths


def solution(mesh):
    return jax.shard_map(
        functools.partial(body, mesh.shape["trade"]),
        mesh=mesh,
        in_specs=(
            P(("group", "trade"), None),
            P(),
            P(("group", "trade"), None),
            P(("group", "trade")),
            P(("group", "trade")),
            P(("group", "trade")),
            P("group"),
            P(("group", "trade")),
            P(("group", "trade"), None),
        ),
        out_specs=P(("group", "trade"), None),
        check_vma=False,
    )
```

```python
import functools

import jax
import jax.numpy as jnp
from jax import lax
from jax.experimental import pallas as pl
from jax.experimental.pallas import tpu as pltpu
from jax.sharding import PartitionSpec as P

F = 16
K = 32
DATES = 8
LAG = 2
LANES = 128
CHUNK = 256
COLS = 512
MESH = pl.DeviceIdType.MESH
f32 = jnp.float32
bf16 = jnp.bfloat16


def iota(shape, axis):
    return lax.broadcasted_iota(jnp.int32, shape, axis)


def plane_size(n):
    return 1 << ((n.bit_length() - 1) // 2)


def kernel(
    n,
    factors,
    loadings,
    trade_coef,
    basis_size,
    set_ids,
    live_count,
    netting_row,
    threshold,
    margin_start,
    out,
    fact,
    load_v,
    coef_v,
    size_v,
    ids_v,
    nrow_v,
    thr_s,
    marg_v,
    split,
    onehot,
    spread,
    basis,
    held,
    acc,
    part,
    recv,
    in_sem,
    gs_sem,
    up_sem,
    near_sem,
    high_sem,
    low_sem,
    ready,
    ss_sem,
    sr_sem,
):
    me = lax.axis_index("trade")
    rows = fact.shape[1]
    paths = n * rows
    rep = max(1, LANES // paths)
    width = rep * paths
    slots = coef_v.shape[0]
    owned = recv.shape[1]
    sets = n * owned

    def peer(k):
        return lax.rem(me + k, n)

    plane = plane_size(n)
    levels = n // plane
    level = lax.div(me, plane)
    spot = lax.rem(me, plane)
    inner = level < levels - 1

    def each_of(low, high, step):
        lax.fori_loop(low, high, lambda j, c: (step(j), c)[1], 0)

    def each_near(step):
        for k in range(1, plane):
            step(level * plane + lax.rem(spot + k, plane))

    def each_peer(step):
        lax.fori_loop(1, n, lambda k, c: (step(peer(k)), c)[1], 0)

    def local(src, dst, i):
        return pltpu.make_async_copy(src, dst, in_sem.at[i])

    def settle(ref, sem, count):
        rest = ref.at[pl.ds(0, count)]
        pltpu.make_async_copy(rest, rest, sem).wait()

    barrier = pltpu.get_barrier_semaphore()

    def greet(j):
        pl.semaphore_signal(barrier, inc=1, device_id={"trade": j}, device_id_type=MESH)

    each_near(greet)
    each_of((level + 1) * plane, n, greet)

    own = local(factors, fact.at[me], 0)
    limit_copy = local(threshold, thr_s, 1)
    pairs = (
        (loadings, load_v),
        (basis_size, size_v),
        (netting_row, nrow_v),
        (set_ids, ids_v),
        (margin_start, marg_v),
        (trade_coef, coef_v),
    )
    copies = [local(src, dst, 2) for src, dst in pairs]
    for copy in (own, *copies, limit_copy):
        copy.start()
    pl.semaphore_wait(barrier, plane - 1 + level * plane)

    @pl.when(level > 0)
    def _():
        pl.semaphore_signal(ready, inc=1, device_id={"trade": me - plane}, device_id_type=MESH)

    def send(j, src, out_sem, sem):
        pltpu.make_async_remote_copy(
            src_ref=src,
            dst_ref=src,
            send_sem=out_sem,
            recv_sem=sem,
            device_id={"trade": j},
            device_id_type=MESH,
        ).start()

    own.wait()
    each_near(lambda j: send(j, fact.at[me], gs_sem, near_sem))
    each_of(0, level * plane, lambda j: send(j, fact.at[me], gs_sem, high_sem))

    for copy in copies:
        copy.wait()
    limit_copy.wait()
    tiled = (iota((F, LANES), 1) % F == iota((F, LANES), 0)).astype(f32).astype(bf16)
    diag = iota((DATES * K, LANES), 0) // K == iota((DATES * K, LANES), 1) // F
    rest = load_v[...]
    for i in range(3):
        piece = rest.astype(bf16)
        rest = rest - piece.astype(f32)
        wide = lax.dot_general(piece, tiled, (((0,), (0,)), ((), ())), preferred_element_type=f32)
        wide = jnp.concatenate([wide] * DATES, axis=0)
        split[i] = jnp.where(diag, wide, 0.0).astype(bf16)
    basis[...] = jnp.zeros(basis.shape, bf16)

    found = nrow_v[...] == iota((sets, sets), 0)
    owner_set = jnp.sum(jnp.where(found, iota((sets, sets), 1), 0).astype(f32), axis=1, keepdims=True)
    owner_set = owner_set.astype(jnp.int32)
    for c in range(slots // CHUNK):
        cut = slice(c * CHUNK, (c + 1) * CHUNK)
        onehot[:, cut] = (ids_v[:, cut] == owner_set).astype(f32).astype(bf16)

    for i in range(LAG):
        held[:, i * paths : (i + 1) * paths] = marg_v[...]

    live_now = live_count[0]
    slot_index = iota(size_v.shape, 0) * LANES + iota(size_v.shape, 1)
    used = jnp.where(slot_index < live_now, size_v[...], 0).astype(f32)
    basis_index = (iota((LANES, LANES), 1) % K).astype(f32)
    for c in range(slots // LANES):
        limit = jnp.broadcast_to(used[c : c + 1], (LANES, LANES)).T
        keep = basis_index < limit
        cut = slice(c * LANES, (c + 1) * LANES)
        for h in range(0, DATES * K, LANES):
            side = slice(h, h + LANES)
            coef_v[cut, side] = jnp.where(keep, coef_v[cut, side].astype(f32), 0.0).astype(bf16)

    def layer(i):
        return fact.at[pl.ds(i * plane, plane)]

    def settle_layer(sem):
        pltpu.make_async_copy(layer(0), layer(0), sem).wait()

    def relay(i):
        @pl.when(inner)
        def _():
            send(me + plane, layer(i), up_sem, low_sem.at[i])

    settle(fact, near_sem, plane - 1)

    @pl.when(inner)
    def _():
        pl.semaphore_wait(ready, 1)

    relay(level)

    def climb(i):
        settle_layer(low_sem.at[level - 1 - i])
        relay(level - 1 - i)

    each_of(0, level, climb)
    for i in range(levels - 1):

        @pl.when(level == i)
        def _():
            settle(fact, high_sem, (levels - 1 - i) * plane)


    for j in range(n):
        block = fact[j].astype(f32)
        for i in range(rep):
            at = i * paths + j * rows
            spread[at : at + rows] = block
    table = spread[...].astype(bf16)
    dims = (((1,), (1,)), ((), ()))
    loaded = lax.dot_general(split[2], table, dims, preferred_element_type=f32)
    loaded += lax.dot_general(split[1], table, dims, preferred_element_type=f32)
    loaded += lax.dot_general(split[0], table, dims, preferred_element_type=f32)
    bent = jnp.tanh(loaded)
    tall = rep * K
    pair = iota((tall, width), 0) // K == iota((tall, width), 1) // paths
    for j in range(DATES // rep):
        strip = jnp.where(pair, bent[j * tall : (j + 1) * tall], 0.0).astype(bf16)
        basis[j * tall : (j + 1) * tall, j * width : (j + 1) * width] = strip

    def block_sums(right):
        total = None
        for c in range(slots // CHUNK):
            cut = slice(c * CHUNK, (c + 1) * CHUNK)
            values = jnp.dot(coef_v[cut], right, preferred_element_type=f32).astype(bf16)
            term = jnp.dot(onehot[:, cut], values, preferred_element_type=f32)
            total = term if total is None else total + term
        return total

    blocks = acc.shape[1] // COLS
    if blocks == 1:
        acc[...] = block_sums(basis[...])
    else:

        def one(b, carry):
            side = pl.ds(pl.multiple_of(b * COLS, COLS), COLS)
            acc[:, side] = block_sums(basis[:, side])
            return carry

        lax.fori_loop(0, blocks, one, 0)
    for j in range(n):
        part[j] = acc[j * owned : (j + 1) * owned]

    def scatter(j):
        return pltpu.make_async_remote_copy(
            src_ref=part.at[j],
            dst_ref=recv.at[me],
            send_sem=ss_sem,
            recv_sem=sr_sem,
            device_id={"trade": j},
            device_id_type=MESH,
        )

    each_peer(lambda j: scatter(j).start())
    recv[me] = part[me]
    settle(recv, sr_sem, n - 1)

    netted = recv[0]
    for j in range(1, n):
        netted = netted + recv[j]
    row_at = iota((owned, 1), 0)
    limits = jnp.zeros((owned, 1), f32)
    for r in range(owned):
        limits = jnp.where(row_at == r, thr_s[r], limits)
    first = LAG * paths
    margin = jnp.maximum(netted[:, : (DATES - LAG) * paths] - limits, 0.0)
    head = jnp.maximum(netted[:, :first] - held[...], 0.0)
    tail = jnp.maximum(netted[:, first:] - margin, 0.0)
    result = jnp.zeros(out.shape, f32)
    lane_date = iota((owned, width), 1) // paths
    column = iota(out.shape, 1)
    for j in range(DATES // rep):
        at = j * width
        block = head[:, at : at + width] if at < first else tail[:, at - first : at - first + width]
        for i in range(rep):
            own = jnp.where(lane_date == i, block, 0.0) if rep > 1 else block
            result = jnp.where(column == j * rep + i, jnp.sum(own, axis=1, keepdims=True), result)
    out[...] = result
    for i in range(levels):

        @pl.when(level == i)
        def _():
            settle(fact, gs_sem, plane - 1 + i * plane)
            if i < levels - 1:
                settle(fact, up_sem, (i + 1) * plane)

    settle(recv, ss_sem, n - 1)


def stay(x):
    return pltpu.with_memory_space_constraint(x, pltpu.MemorySpace.HBM)


def body(n, factors, loadings, trade_coef, basis_size, set_ids, live_count, netting_row, threshold, margin_start):
    rows = factors.shape[0]
    paths = n * rows
    rep = max(1, LANES // paths)
    slots = trade_coef.shape[0]
    sets = netting_row.shape[0]
    owned = threshold.shape[0]
    wide = DATES * paths
    hbm = pl.BlockSpec(memory_space=pltpu.MemorySpace.HBM)
    total = pl.pallas_call(
        functools.partial(kernel, n),
        out_shape=jax.ShapeDtypeStruct((owned, DATES), f32),
        in_specs=[hbm] * 5 + [pl.BlockSpec(memory_space=pltpu.SMEM)] + [hbm] * 3,
        out_specs=pl.BlockSpec(memory_space=pltpu.VMEM),
        scratch_shapes=[
            pltpu.VMEM((n, rows, DATES * F), bf16),
            pltpu.VMEM((F, K), f32),
            pltpu.VMEM((slots, DATES * K), bf16),
            pltpu.VMEM((slots // LANES, LANES), jnp.int32),
            pltpu.VMEM((1, slots), jnp.int32),
            pltpu.VMEM((1, sets), jnp.int32),
            pltpu.SMEM((owned,), f32),
            pltpu.VMEM((owned, paths), f32),
            pltpu.VMEM((3, DATES * K, DATES * F), bf16),
            pltpu.VMEM((sets, slots), bf16),
            pltpu.VMEM((rep * paths, DATES * F), f32),
            pltpu.VMEM((DATES * K, wide), bf16),
            pltpu.VMEM((owned, LAG * paths), f32),
            pltpu.VMEM((sets, wide), f32),
            pltpu.VMEM((n, owned, wide), f32),
            pltpu.VMEM((n, owned, wide), f32),
            pltpu.SemaphoreType.DMA((3,)),
            pltpu.SemaphoreType.DMA,
            pltpu.SemaphoreType.DMA,
            pltpu.SemaphoreType.DMA,
            pltpu.SemaphoreType.DMA,
            pltpu.SemaphoreType.DMA((n // plane_size(n),)),
            pltpu.SemaphoreType.REGULAR,
            pltpu.SemaphoreType.DMA,
            pltpu.SemaphoreType.DMA,
        ],
        compiler_params=pltpu.CompilerParams(
            collective_id=0, has_side_effects=True, vmem_limit_bytes=48 * 2**20
        ),
    )(
        stay(factors),
        stay(loadings.T),
        stay(trade_coef),
        stay(basis_size.reshape(slots // LANES, LANES)),
        stay(set_ids.reshape(1, slots)),
        live_count,
        stay(netting_row.reshape(1, sets)),
        stay(threshold),
        stay(margin_start),
    )
    return total / paths


def solution(mesh):
    return jax.shard_map(
        functools.partial(body, mesh.shape["trade"]),
        mesh=mesh,
        in_specs=(
            P(("group", "trade"), None),
            P(),
            P(("group", "trade"), None),
            P(("group", "trade")),
            P(("group", "trade")),
            P(("group", "trade")),
            P("group"),
            P(("group", "trade")),
            P(("group", "trade"), None),
        ),
        out_specs=P(("group", "trade"), None),
        check_vma=False,
    )
```

```python
import functools

import jax
import jax.numpy as jnp
from jax import lax
from jax.experimental import pallas as pl
from jax.experimental.pallas import tpu as pltpu
from jax.sharding import PartitionSpec as P

F = 16
K = 32
DATES = 8
LAG = 2
LANES = 128
CHUNK = 256
COLS = 512
MESH = pl.DeviceIdType.MESH
f32 = jnp.float32
bf16 = jnp.bfloat16


def iota(shape, axis):
    return lax.broadcasted_iota(jnp.int32, shape, axis)


def kernel(
    n,
    factors,
    loadings,
    trade_coef,
    basis_size,
    set_ids,
    live_count,
    netting_row,
    threshold,
    margin_start,
    out,
    fact,
    load_v,
    coef_v,
    size_v,
    ids_v,
    nrow_v,
    thr_s,
    marg_v,
    split,
    onehot,
    spread,
    basis,
    held,
    acc,
    part,
    recv,
    in_sem,
    gs_sem,
    gr_sem,
    ss_sem,
    sr_sem,
):
    me = lax.axis_index("trade")
    rows = fact.shape[1]
    paths = n * rows
    rep = max(1, LANES // paths)
    width = rep * paths
    slots = coef_v.shape[0]
    owned = recv.shape[1]
    sets = n * owned

    def each_peer(step, last_first=False):
        def at(i):
            i = n - 2 - i if last_first else i
            step(jnp.where(i >= me, i + 1, i))

        if n <= LANES // 4:
            for i in range(n - 1):
                at(i)
        else:
            lax.fori_loop(0, n - 1, lambda i, c: (at(i), c)[1], 0)

    def local(src, dst, i):
        return pltpu.make_async_copy(src, dst, in_sem.at[i])

    def settle(ref, sem):
        rest = ref.at[pl.ds(0, n - 1)]
        pltpu.make_async_copy(rest, rest, sem).wait()

    barrier = pltpu.get_barrier_semaphore()
    each_peer(lambda j: pl.semaphore_signal(barrier, inc=1, device_id={"trade": j}, device_id_type=MESH))

    own = local(factors, fact.at[me], 0)
    limit_copy = local(threshold, thr_s, 1)
    pairs = (
        (loadings, load_v),
        (basis_size, size_v),
        (netting_row, nrow_v),
        (set_ids, ids_v),
        (margin_start, marg_v),
        (trade_coef, coef_v),
    )
    copies = [local(src, dst, 2) for src, dst in pairs]
    for copy in (own, *copies, limit_copy):
        copy.start()
    own.wait()
    pl.semaphore_wait(barrier, n - 1)

    def gather(j):
        return pltpu.make_async_remote_copy(
            src_ref=fact.at[me],
            dst_ref=fact.at[me],
            send_sem=gs_sem,
            recv_sem=gr_sem,
            device_id={"trade": j},
            device_id_type=MESH,
        )

    each_peer(lambda j: gather(j).start(), last_first=True)

    for copy in copies:
        copy.wait()
    limit_copy.wait()
    tiled = (iota((F, LANES), 1) % F == iota((F, LANES), 0)).astype(f32).astype(bf16)
    diag = iota((DATES * K, LANES), 0) // K == iota((DATES * K, LANES), 1) // F
    rest = load_v[...]
    for i in range(3):
        piece = rest.astype(bf16)
        rest = rest - piece.astype(f32)
        wide = lax.dot_general(piece, tiled, (((0,), (0,)), ((), ())), preferred_element_type=f32)
        wide = jnp.concatenate([wide] * DATES, axis=0)
        split[i] = jnp.where(diag, wide, 0.0).astype(bf16)
    basis[...] = jnp.zeros(basis.shape, bf16)

    found = nrow_v[...] == iota((sets, sets), 0)
    owner_set = jnp.sum(jnp.where(found, iota((sets, sets), 1), 0).astype(f32), axis=1, keepdims=True)
    owner_set = owner_set.astype(jnp.int32)
    for c in range(slots // CHUNK):
        cut = slice(c * CHUNK, (c + 1) * CHUNK)
        onehot[:, cut] = (ids_v[:, cut] == owner_set).astype(f32).astype(bf16)

    for i in range(LAG):
        held[:, i * paths : (i + 1) * paths] = marg_v[...]

    live_now = live_count[0]
    slot_index = iota(size_v.shape, 0) * LANES + iota(size_v.shape, 1)
    used = jnp.where(slot_index < live_now, size_v[...], 0).astype(f32)
    basis_index = (iota((LANES, LANES), 1) % K).astype(f32)
    for c in range(slots // LANES):
        limit = jnp.broadcast_to(used[c : c + 1], (LANES, LANES)).T
        keep = basis_index < limit
        cut = slice(c * LANES, (c + 1) * LANES)
        for h in range(0, DATES * K, LANES):
            side = slice(h, h + LANES)
            coef_v[cut, side] = jnp.where(keep, coef_v[cut, side].astype(f32), 0.0).astype(bf16)

    settle(fact, gr_sem)

    for j in range(n):
        block = fact[j].astype(f32)
        for i in range(rep):
            at = i * paths + j * rows
            spread[at : at + rows] = block
    table = spread[...].astype(bf16)
    dims = (((1,), (1,)), ((), ()))
    loaded = lax.dot_general(split[2], table, dims, preferred_element_type=f32)
    loaded += lax.dot_general(split[1], table, dims, preferred_element_type=f32)
    loaded += lax.dot_general(split[0], table, dims, preferred_element_type=f32)
    bent = jnp.tanh(loaded)
    tall = rep * K
    pair = iota((tall, width), 0) // K == iota((tall, width), 1) // paths
    for j in range(DATES // rep):
        strip = jnp.where(pair, bent[j * tall : (j + 1) * tall], 0.0).astype(bf16)
        basis[j * tall : (j + 1) * tall, j * width : (j + 1) * width] = strip

    def block_sums(right):
        total = None
        for c in range(slots // CHUNK):
            cut = slice(c * CHUNK, (c + 1) * CHUNK)
            values = jnp.dot(coef_v[cut], right, preferred_element_type=f32).astype(bf16)
            term = jnp.dot(onehot[:, cut], values, preferred_element_type=f32)
            total = term if total is None else total + term
        return total

    blocks = acc.shape[1] // COLS
    if blocks == 1:
        acc[...] = block_sums(basis[...])
    else:

        def one(b, carry):
            side = pl.ds(pl.multiple_of(b * COLS, COLS), COLS)
            acc[:, side] = block_sums(basis[:, side])
            return carry

        lax.fori_loop(0, blocks, one, 0)
    for j in range(n):
        part[j] = acc[j * owned : (j + 1) * owned]

    def scatter(j):
        return pltpu.make_async_remote_copy(
            src_ref=part.at[j],
            dst_ref=recv.at[me],
            send_sem=ss_sem,
            recv_sem=sr_sem,
            device_id={"trade": j},
            device_id_type=MESH,
        )

    each_peer(lambda j: scatter(j).start())
    recv[me] = part[me]
    settle(recv, sr_sem)

    netted = recv[0]
    for j in range(1, n):
        netted = netted + recv[j]
    row_at = iota((owned, 1), 0)
    limits = jnp.zeros((owned, 1), f32)
    for r in range(owned):
        limits = jnp.where(row_at == r, thr_s[r], limits)
    first = LAG * paths
    margin = jnp.maximum(netted[:, : (DATES - LAG) * paths] - limits, 0.0)
    head = jnp.maximum(netted[:, :first] - held[...], 0.0)
    tail = jnp.maximum(netted[:, first:] - margin, 0.0)
    result = jnp.zeros(out.shape, f32)
    lane_date = iota((owned, width), 1) // paths
    column = iota(out.shape, 1)
    for j in range(DATES // rep):
        at = j * width
        block = head[:, at : at + width] if at < first else tail[:, at - first : at - first + width]
        for i in range(rep):
            own = jnp.where(lane_date == i, block, 0.0) if rep > 1 else block
            result = jnp.where(column == j * rep + i, jnp.sum(own, axis=1, keepdims=True), result)
    out[...] = result
    settle(fact, gs_sem)
    settle(recv, ss_sem)


def stay(x):
    return pltpu.with_memory_space_constraint(x, pltpu.MemorySpace.HBM)


def body(n, factors, loadings, trade_coef, basis_size, set_ids, live_count, netting_row, threshold, margin_start):
    rows = factors.shape[0]
    paths = n * rows
    rep = max(1, LANES // paths)
    slots = trade_coef.shape[0]
    sets = netting_row.shape[0]
    owned = threshold.shape[0]
    wide = DATES * paths
    hbm = pl.BlockSpec(memory_space=pltpu.MemorySpace.HBM)
    total = pl.pallas_call(
        functools.partial(kernel, n),
        out_shape=jax.ShapeDtypeStruct((owned, DATES), f32),
        in_specs=[hbm] * 5 + [pl.BlockSpec(memory_space=pltpu.SMEM)] + [hbm] * 3,
        out_specs=pl.BlockSpec(memory_space=pltpu.VMEM),
        scratch_shapes=[
            pltpu.VMEM((n, rows, DATES * F), bf16),
            pltpu.VMEM((F, K), f32),
            pltpu.VMEM((slots, DATES * K), bf16),
            pltpu.VMEM((slots // LANES, LANES), jnp.int32),
            pltpu.VMEM((1, slots), jnp.int32),
            pltpu.VMEM((1, sets), jnp.int32),
            pltpu.SMEM((owned,), f32),
            pltpu.VMEM((owned, paths), f32),
            pltpu.VMEM((3, DATES * K, DATES * F), bf16),
            pltpu.VMEM((sets, slots), bf16),
            pltpu.VMEM((rep * paths, DATES * F), f32),
            pltpu.VMEM((DATES * K, wide), bf16),
            pltpu.VMEM((owned, LAG * paths), f32),
            pltpu.VMEM((sets, wide), f32),
            pltpu.VMEM((n, owned, wide), f32),
            pltpu.VMEM((n, owned, wide), f32),
            pltpu.SemaphoreType.DMA((3,)),
            pltpu.SemaphoreType.DMA,
            pltpu.SemaphoreType.DMA,
            pltpu.SemaphoreType.DMA,
            pltpu.SemaphoreType.DMA,
        ],
        compiler_params=pltpu.CompilerParams(
            collective_id=0, has_side_effects=True, vmem_limit_bytes=48 * 2**20
        ),
    )(
        stay(factors),
        stay(loadings.T),
        stay(trade_coef),
        stay(basis_size.reshape(slots // LANES, LANES)),
        stay(set_ids.reshape(1, slots)),
        live_count,
        stay(netting_row.reshape(1, sets)),
        stay(threshold),
        stay(margin_start),
    )
    return total / paths


def solution(mesh):
    return jax.shard_map(
        functools.partial(body, mesh.shape["trade"]),
        mesh=mesh,
        in_specs=(
            P(("group", "trade"), None),
            P(),
            P(("group", "trade"), None),
            P(("group", "trade")),
            P(("group", "trade")),
            P(("group", "trade")),
            P("group"),
            P(("group", "trade")),
            P(("group", "trade"), None),
        ),
        out_specs=P(("group", "trade"), None),
        check_vma=False,
    )
```

```python
import functools

import jax
import jax.numpy as jnp
from jax import lax
from jax.experimental import pallas as pl
from jax.experimental.pallas import tpu as pltpu
from jax.sharding import PartitionSpec as P

F = 16
K = 32
DATES = 8
LAG = 2
LANES = 128
CHUNK = 256
COLS = 512
MESH = pl.DeviceIdType.MESH
f32 = jnp.float32
bf16 = jnp.bfloat16


def iota(shape, axis):
    return lax.broadcasted_iota(jnp.int32, shape, axis)


def kernel(
    n,
    factors,
    loadings,
    trade_coef,
    basis_size,
    set_ids,
    live_count,
    netting_row,
    threshold,
    margin_start,
    out,
    fact,
    load_v,
    coef_v,
    size_v,
    ids_v,
    nrow_v,
    thr_s,
    marg_v,
    split,
    onehot,
    spread,
    basis,
    held,
    acc,
    part,
    recv,
    in_sem,
    gs_sem,
    gr_sem,
    ss_sem,
    sr_sem,
):
    me = lax.axis_index("trade")
    rows = fact.shape[1]
    near = n // 2
    paths = near * rows
    rep = max(1, LANES // paths)
    width = rep * paths
    slots = coef_v.shape[0]
    owned = recv.shape[2]
    mine = lax.div(me, near)
    sets = n * owned

    def each_peer(step, last_first=False):
        def at(i):
            i = n - 2 - i if last_first else i
            step(jnp.where(i >= me, i + 1, i))

        if n <= LANES // 4:
            for i in range(n - 1):
                at(i)
        else:
            lax.fori_loop(0, n - 1, lambda i, c: (at(i), c)[1], 0)

    def local(src, dst, i):
        return pltpu.make_async_copy(src, dst, in_sem.at[i])

    def settle(ref, sem, count):
        rest = ref.at[pl.ds(0, count)]
        pltpu.make_async_copy(rest, rest, sem).wait()

    barrier = pltpu.get_barrier_semaphore()
    each_peer(lambda j: pl.semaphore_signal(barrier, inc=1, device_id={"trade": j}, device_id_type=MESH))

    own = local(factors, fact.at[me], 0)
    limit_copy = local(threshold, thr_s, 1)
    pairs = (
        (loadings, load_v),
        (basis_size, size_v),
        (netting_row, nrow_v),
        (set_ids, ids_v),
        (margin_start, marg_v),
        (trade_coef, coef_v),
    )
    copies = [local(src, dst, 2) for src, dst in pairs]
    for copy in (own, *copies, limit_copy):
        copy.start()
    own.wait()
    pl.semaphore_wait(barrier, n - 1)

    def gather(j):
        return pltpu.make_async_remote_copy(
            src_ref=fact.at[me],
            dst_ref=fact.at[me],
            send_sem=gs_sem,
            recv_sem=gr_sem.at[mine],
            device_id={"trade": j},
            device_id_type=MESH,
        )

    each_peer(lambda j: gather(j).start(), last_first=True)

    for copy in copies:
        copy.wait()
    limit_copy.wait()
    tiled = (iota((F, LANES), 1) % F == iota((F, LANES), 0)).astype(f32).astype(bf16)
    diag = iota((DATES * K, LANES), 0) // K == iota((DATES * K, LANES), 1) // F
    rest = load_v[...]
    for i in range(3):
        piece = rest.astype(bf16)
        rest = rest - piece.astype(f32)
        wide = lax.dot_general(piece, tiled, (((0,), (0,)), ((), ())), preferred_element_type=f32)
        wide = jnp.concatenate([wide] * DATES, axis=0)
        split[i] = jnp.where(diag, wide, 0.0).astype(bf16)
    basis[...] = jnp.zeros(basis.shape, bf16)

    found = nrow_v[...] == iota((sets, sets), 0)
    owner_set = jnp.sum(jnp.where(found, iota((sets, sets), 1), 0).astype(f32), axis=1, keepdims=True)
    owner_set = owner_set.astype(jnp.int32)
    for c in range(slots // CHUNK):
        cut = slice(c * CHUNK, (c + 1) * CHUNK)
        onehot[:, cut] = (ids_v[:, cut] == owner_set).astype(f32).astype(bf16)

    for half in range(2):
        for i in range(LAG):
            held[half, :, i * paths : (i + 1) * paths] = marg_v[:, half * paths : (half + 1) * paths]

    live_now = live_count[0]
    slot_index = iota(size_v.shape, 0) * LANES + iota(size_v.shape, 1)
    used = jnp.where(slot_index < live_now, size_v[...], 0).astype(f32)
    basis_index = (iota((LANES, LANES), 1) % K).astype(f32)
    for c in range(slots // LANES):
        limit = jnp.broadcast_to(used[c : c + 1], (LANES, LANES)).T
        keep = basis_index < limit
        cut = slice(c * LANES, (c + 1) * LANES)
        for h in range(0, DATES * K, LANES):
            side = slice(h, h + LANES)
            coef_v[cut, side] = jnp.where(keep, coef_v[cut, side].astype(f32), 0.0).astype(bf16)

    def half_sums(half):
        for j in range(near):
            block = fact[half * near + j].astype(f32)
            for i in range(rep):
                at = i * paths + j * rows
                spread[at : at + rows] = block
        table = spread[...].astype(bf16)
        dims = (((1,), (1,)), ((), ()))
        loaded = lax.dot_general(split[2], table, dims, preferred_element_type=f32)
        loaded += lax.dot_general(split[1], table, dims, preferred_element_type=f32)
        loaded += lax.dot_general(split[0], table, dims, preferred_element_type=f32)
        bent = jnp.tanh(loaded)
        tall = rep * K
        pair = iota((tall, width), 0) // K == iota((tall, width), 1) // paths
        for j in range(DATES // rep):
            strip = jnp.where(pair, bent[j * tall : (j + 1) * tall], 0.0).astype(bf16)
            basis[j * tall : (j + 1) * tall, j * width : (j + 1) * width] = strip

        def block_sums(right):
            total = None
            for c in range(slots // CHUNK):
                cut = slice(c * CHUNK, (c + 1) * CHUNK)
                values = jnp.dot(coef_v[cut], right, preferred_element_type=f32).astype(bf16)
                term = jnp.dot(onehot[:, cut], values, preferred_element_type=f32)
                total = term if total is None else total + term
            return total

        blocks = max(1, acc.shape[1] // COLS)
        if blocks == 1:
            acc[...] = block_sums(basis[...])
        else:

            def one(b, carry):
                side = pl.ds(pl.multiple_of(b * COLS, COLS), COLS)
                acc[:, side] = block_sums(basis[:, side])
                return carry

            lax.fori_loop(0, blocks, one, 0)
        for j in range(n):
            part[half, j] = acc[j * owned : (j + 1) * owned]

    def scatter(j, half, stage):
        return pltpu.make_async_remote_copy(
            src_ref=part.at[half, j],
            dst_ref=recv.at[half, me],
            send_sem=ss_sem.at[stage],
            recv_sem=sr_sem.at[half],
            device_id={"trade": j},
            device_id_type=MESH,
        )

    settle(fact, gr_sem.at[mine], near - 1)
    half_sums(mine)
    each_peer(lambda j: scatter(j, mine, 0).start())
    settle(fact, gr_sem.at[1 - mine], near)
    half_sums(1 - mine)
    each_peer(lambda j: scatter(j, 1 - mine, 1).start())
    for half in range(2):
        recv[half, me] = part[half, me]
    settle(recv.at[0], sr_sem.at[0], n - 1)
    settle(recv.at[1], sr_sem.at[1], n - 1)

    row_at = iota((owned, 1), 0)
    limits = jnp.zeros((owned, 1), f32)
    for r in range(owned):
        limits = jnp.where(row_at == r, thr_s[r], limits)
    first = LAG * paths
    result = jnp.zeros(out.shape, f32)
    lane_date = iota((owned, width), 1) // paths
    column = iota(out.shape, 1)
    short = jnp.zeros((owned, DATES * paths), f32)
    for half in range(2):
        netted = recv[half, 0]
        for j in range(1, n):
            netted = netted + recv[half, j]
        margin = jnp.maximum(netted[:, : (DATES - LAG) * paths] - limits, 0.0)
        collateral = jnp.concatenate([held[half], margin], axis=1)
        short = short + jnp.maximum(netted - collateral, 0.0)
    for j in range(DATES // rep):
        block = short[:, j * width : (j + 1) * width]
        for i in range(rep):
            own_date = jnp.where(lane_date == i, block, 0.0) if rep > 1 else block
            result = jnp.where(column == j * rep + i, jnp.sum(own_date, axis=1, keepdims=True), result)
    out[...] = result
    settle(fact, gs_sem, n - 1)
    settle(recv.at[0], ss_sem.at[0], n - 1)
    settle(recv.at[1], ss_sem.at[1], n - 1)


def stay(x):
    return pltpu.with_memory_space_constraint(x, pltpu.MemorySpace.HBM)


def body(n, factors, loadings, trade_coef, basis_size, set_ids, live_count, netting_row, threshold, margin_start):
    rows = factors.shape[0]
    paths = n * rows
    half = paths // 2
    rep = max(1, LANES // half)
    slots = trade_coef.shape[0]
    sets = netting_row.shape[0]
    owned = threshold.shape[0]
    wide = DATES * half
    hbm = pl.BlockSpec(memory_space=pltpu.MemorySpace.HBM)
    total = pl.pallas_call(
        functools.partial(kernel, n),
        out_shape=jax.ShapeDtypeStruct((owned, DATES), f32),
        in_specs=[hbm] * 5 + [pl.BlockSpec(memory_space=pltpu.SMEM)] + [hbm] * 3,
        out_specs=pl.BlockSpec(memory_space=pltpu.VMEM),
        scratch_shapes=[
            pltpu.VMEM((n, rows, DATES * F), bf16),
            pltpu.VMEM((F, K), f32),
            pltpu.VMEM((slots, DATES * K), bf16),
            pltpu.VMEM((slots // LANES, LANES), jnp.int32),
            pltpu.VMEM((1, slots), jnp.int32),
            pltpu.VMEM((1, sets), jnp.int32),
            pltpu.SMEM((owned,), f32),
            pltpu.VMEM((owned, paths), f32),
            pltpu.VMEM((3, DATES * K, DATES * F), bf16),
            pltpu.VMEM((sets, slots), bf16),
            pltpu.VMEM((rep * half, DATES * F), f32),
            pltpu.VMEM((DATES * K, wide), bf16),
            pltpu.VMEM((2, owned, LAG * half), f32),
            pltpu.VMEM((sets, wide), f32),
            pltpu.VMEM((2, n, owned, wide), f32),
            pltpu.VMEM((2, n, owned, wide), f32),
            pltpu.SemaphoreType.DMA((3,)),
            pltpu.SemaphoreType.DMA,
            pltpu.SemaphoreType.DMA((2,)),
            pltpu.SemaphoreType.DMA((2,)),
            pltpu.SemaphoreType.DMA((2,)),
        ],
        compiler_params=pltpu.CompilerParams(
            collective_id=0, has_side_effects=True, vmem_limit_bytes=48 * 2**20
        ),
    )(
        stay(factors),
        stay(loadings.T),
        stay(trade_coef),
        stay(basis_size.reshape(slots // LANES, LANES)),
        stay(set_ids.reshape(1, slots)),
        live_count,
        stay(netting_row.reshape(1, sets)),
        stay(threshold),
        stay(margin_start),
    )
    return total / paths


def solution(mesh):
    return jax.shard_map(
        functools.partial(body, mesh.shape["trade"]),
        mesh=mesh,
        in_specs=(
            P(("group", "trade"), None),
            P(),
            P(("group", "trade"), None),
            P(("group", "trade")),
            P(("group", "trade")),
            P(("group", "trade")),
            P("group"),
            P(("group", "trade")),
            P(("group", "trade"), None),
        ),
        out_specs=P(("group", "trade"), None),
        check_vma=False,
    )
```
